512 devices in a mesh: row: 32 (over z, y_lo, core), col: 16 (over y_hi, x).
Axes of the slice: x: 4, y: 8 (y_hi: 4, y_lo: 2; y = y_hi * 2 + y_lo), z: 8, core: 2. Of those that a mesh axis runs over, the one named last changes fastest.
Arguments:
- r_vals: bfloat16 [65536, 2048], P('row', 'col'), may hold values from -6 to 6
- s_vals: bfloat16 [2048, 4096], P('row', 'col'), may hold values from -0.125 to 0.125
- t_vals: bfloat16 [4096, 65536], P(None, ('row', 'col')), may hold values from -6 to 6
- r_pattern: int32 [512, 16], replicated, may hold values 0 or 1
- s_pattern: int32 [16, 32], replicated, may hold values 0 or 1
- t_pattern: int32 [32, 512], replicated, may hold values 0 or 1
Outputs:
- joined: bfloat16 [65536, 4096], P('row', 'col')
The draws below stay inside these ranges and needn't reach their ends.
All inputs are finite; a program needn't handle non-finite values.
Results may differ from the reference program's by a relative error of at most 0.001.
Values may be sent and summed in bfloat16 or wider, within the bound.
A program may use at most 64 MiB of HBM per device.

```python
import jax
import jax.numpy as jnp
from jax import lax

BLK = 128
TI = 16
KT = 16
NA = 65536
NB = 2048
NC = 4096
TA = 512
TC = 32
N_ROW = 32


def touch_ends(entries, key, smallest, top_value):
    longest = entries.shape.index(max(entries.shape))
    spots = []
    for shift in (0, 1):
        where = [jax.random.randint(jax.random.fold_in(key, axis), (), 0, length) for axis, length in enumerate(entries.shape)]
        where[longest] = (where[longest] + shift) % entries.shape[longest]
        spots.append(tuple(where))
    return entries.at[spots[0]].set(smallest).at[spots[1]].set(top_value)


def block_levels(key, dims, cuts, least, high):
    def one(axis_at, blocks):
        draws = jax.random.uniform(jax.random.fold_in(jax.random.fold_in(key, 6), axis_at), (blocks,), jnp.float32, least / len(cuts), high / len(cuts))
        return jnp.repeat(jnp.exp(draws), dims[axis_at] // blocks).reshape((-1,) + (1,) * (len(dims) - axis_at - 1))

    gain = one(*cuts[0])
    for cut in cuts[1:]:
        gain = gain * one(*cut)
    return gain


def normal_values(key, extent, scale, bound, split=(), dtype=jnp.bfloat16):
    result = scale * jax.random.normal(key, extent, jnp.float32)
    if split:
        result = result * block_levels(key, extent, split, -0.22, 0.18)
    return jnp.clip(result, -bound, bound).astype(dtype)


def setup_inputs(seed: int = 0) -> dict:
    key_of = jax.random.split(jax.random.key(seed), 7)
    return {
        "r_vals": normal_values(key_of[0], (NA, NB), 1.0, 6.0, ((0, 32), (1, 16))),
        "s_vals": normal_values(key_of[1], (NB, NC), NB ** -0.5, 0.125, ((0, 32), (1, 16))),
        "t_vals": normal_values(key_of[2], (NC, NA), 1.0, 6.0, ((1, 512),)),
        "r_pattern": touch_ends((jax.random.randint(key_of[3], (TA, KT), 0, 3) < 2).astype(jnp.int32), jax.random.fold_in(key_of[3], 1), 0, 1),
        "s_pattern": touch_ends((jax.random.randint(key_of[4], (KT, TC), 0, 3) < 2).astype(jnp.int32), jax.random.fold_in(key_of[4], 1), 0, 1),
        "t_pattern": touch_ends((jax.random.randint(key_of[5], (TC, TA), 0, 3) < 2).astype(jnp.int32), jax.random.fold_in(key_of[5], 1), 0, 1),
    }


def tile_apply(values, pattern):
    tile_rows, tile_cols = pattern.shape
    blocks = values.astype(jnp.float32).reshape(tile_rows, BLK, tile_cols, BLK)
    blocks = blocks * pattern.astype(jnp.float32)[:, None, :, None]
    return blocks.reshape(values.shape).astype(jnp.bfloat16)


def reference(r_vals, s_vals, t_vals, r_pattern, s_pattern, t_pattern):
    r_eff = tile_apply(r_vals, r_pattern)
    s_eff = tile_apply(s_vals, s_pattern)
    t_eff = tile_apply(t_vals, t_pattern)
    row_blocks = r_eff.reshape(N_ROW, TI * BLK, NB)
    t_blocks = jnp.transpose(t_eff.reshape(NC, N_ROW, TI * BLK), (1, 2, 0))

    def one_block(pair):
        left, mirror = pair
        paths = jnp.dot(left, s_eff, preferred_element_type=jnp.float32)
        return (paths * mirror.astype(jnp.float32)).astype(jnp.bfloat16)

    joined = lax.map(one_block, (row_blocks, t_blocks))
    return joined.reshape(NA, NC)
```

```python
import jax
import jax.numpy as jnp
from jax import lax
from jax.experimental import pallas as pl
from jax.experimental.pallas import tpu as pltpu
from jax.sharding import PartitionSpec as P

MESH = pl.DeviceIdType.MESH
BLK = 128
PASSES = 2
H = 512 // PASSES
SEMS = 144


def kernel(
    r_ref, s_ref, t_ref, rp_ref, sp_ref, tp_ref, out_ref,
    rbuf, rrel, sbuf, tbuf, trel, obuf, orel, reff, seff, rp, sp, tp, ssem, rsem, lsem,
):
    row, col = lax.axis_index("row"), lax.axis_index("col")
    z, yl, core = lax.div(row, 4), lax.rem(lax.div(row, 2), 2), lax.rem(row, 2)
    yh, x = lax.div(col, 4), lax.rem(col, 4)
    xs = [lax.rem(x + d, 4) for d in range(4)]
    ys = [lax.rem(yh + d, 4) for d in range(4)]
    zs = [lax.rem(z + d, 8) for d in range(8)]
    low = yl * 2 + core
    x_to = [(row, yh * 4 + xs[1]), (row, yh * 4 + xs[3])]
    y_to = [(row, ys[1] * 4 + x), (row, ys[3] * 4 + x)]
    z_to = [(zs[1] * 4 + low, col), (zs[7] * 4 + low, col)]
    pair = (z * 4 + (1 - yl) * 2 + core, col)
    twin = (row + 1 - 2 * core, col)
    par = lax.rem(yh, 2)
    pars = [1 - par, par]
    block = [yh, ys[1], ys[3], ys[2]]
    half = [pl.ds(0, H // 2), pl.ds(H // 2, H // 2)]

    sent = {}

    def send(name, src, dst, device):
        n = len(sent)
        sent[name] = pltpu.make_async_remote_copy(
            src_ref=src, dst_ref=dst, send_sem=ssem.at[n], recv_sem=rsem.at[n],
            device_id=device, device_id_type=MESH,
        )
        sent[name].start()

    def arrive(*name):
        sent[name].wait_recv()

    local = []

    def fetch(src, dst):
        local.append(pltpu.make_async_copy(src, dst, lsem.at[len(local)]))
        local[-1].start()
        return local[-1]

    barrier = pltpu.get_barrier_semaphore()
    for device in (*x_to, *y_to, *z_to, pair, twin):
        pl.semaphore_signal(barrier, inc=1, device_id=device, device_id_type=MESH)
    own_s = fetch(s_ref, sbuf.at[yh, core, z, yl])
    own_r = [fetch(r_ref.at[yh, p], rbuf.at[col, p]) for p in range(PASSES)]
    own_t = [fetch(t_ref.at[:, pars[ph], x], tbuf.at[ph, x]) for ph in range(2)]
    masks = [
        fetch(rp_ref.at[pl.ds(pl.multiple_of(row * 16, 16), 16)], rp),
        fetch(sp_ref, sp),
        fetch(tp_ref.at[:, pl.ds(pl.multiple_of(lax.div(row, 8) * 128, 128), 128)], tp),
    ]
    pl.semaphore_wait(barrier, 8)

    def r_legs(p):
        for d in range(2):
            send(("RL1", p, d), r_ref.at[ys[2], p, half[d]], rrel.at[p, d], y_to[d])

    def r_direct(p):
        for d in range(2):
            send(("RY", p, d), r_ref.at[ys[(1, 3)[d]], p], rbuf.at[col, p], y_to[d])

    def r_relay(p):
        for d in range(2):
            arrive("RL1", p, d)
            origin = ys[(3, 1)[d]] * 4 + x
            send(("RL2", p, d), rrel.at[p, d], rbuf.at[origin, p, half[d]], y_to[d])

    def r_own(p):
        for d in range(2):
            send(("RX", 0, p, d), r_ref.at[yh, p], rbuf.at[col, p], x_to[d])

    def r_across(j, p):
        chunk = ys[(0, 3, 1, 2)[j]] * 4 + x
        for d in range(2):
            send(("RX", j, p, d), rbuf.at[chunk, p], rbuf.at[chunk, p], x_to[d])

    def r_onward(j, p):
        for d in range(2):
            arrive("RX", j, p, d)
            chunk = ys[(0, 3, 1, 2)[j]] * 4 + xs[(3, 1)[d]]
            part = rbuf.at[chunk, p, half[d]]
            send(("RF", j, p, d), part, part, x_to[d])

    def t_start(ph):
        for d in range(2):
            rows = pl.ds(d * 128, 128)
            send(("TL1", ph, d), t_ref.at[:, pars[ph], xs[2], rows], trel.at[ph, d], x_to[d])
        for d in range(2):
            send(("TD", ph, d), t_ref.at[:, pars[ph], xs[(1, 3)[d]]], tbuf.at[ph, x], x_to[d])

    def t_relay(ph):
        for d in range(2):
            arrive("TL1", ph, d)
            rows = pl.ds(d * 128, 128)
            send(("TL2", ph, d), trel.at[ph, d], tbuf.at[ph, xs[(3, 1)[d]], :, rows], x_to[d])

    def t_done(ph):
        own_t[ph].wait()
        for d in range(2):
            arrive("TD", ph, d)
            arrive("TL2", ph, d)

    def z_send(o, s):
        for d in range(2):
            if s:
                arrive("Z", o, s - 1, d)
            part = sbuf.at[block[o], core, zs[(-s, s)[d]]]
            if s == 3:
                part = part.at[d]
            send(("Z", o, s, d), part, part, z_to[d])

    def s_share(o):
        for d in range(2):
            arrive("Z", o, 3, d)
        part = sbuf.at[block[o], core]
        send(("SC", o), part, part, twin)

    def s_ready(o):
        arrive("SC", o)
        j = (block[o] * 4 + x) * 2
        for k in range(16):
            for c in range(2):
                m = jnp.full((64, 128), sp[k, j + c].astype(jnp.float32)).astype(jnp.bfloat16)
                for b in range(2):
                    seff[o, k * 128 + b * 64 : k * 128 + b * 64 + 64, c * 128 : c * 128 + 128] = (
                        sbuf[block[o], b, k // 2, k % 2, :, c * 128 : c * 128 + 128] * m
                    )

    def r_ready(p):
        for j in range(4):
            for d in range(2):
                arrive("RF", j, p, d)
        for q in range(H // BLK):
            rows = slice(q * BLK, q * BLK + BLK)
            for k in range(16):
                m = rp[yh * 4 + p * (H // BLK) + q, k].astype(jnp.float32)
                m = jnp.full((BLK, BLK), m).astype(jnp.bfloat16)
                reff[p, rows, k * BLK : k * BLK + BLK] = rbuf[k, p, rows] * m

    def compute(p, o, dst):
        ph = 1 if o in (0, 3) else 0
        i = lax.div(block[o], 2)
        paths = jnp.dot(reff[p], seff[o], preferred_element_type=jnp.float32)
        for h in range(H // BLK):
            q = p * (H // BLK) + h
            for c in range(2):
                m = tp[(block[o] * 4 + x) * 2 + c, lax.rem(row, 8) * 16 + yh * 4 + q]
                t = tbuf[ph, q, i, c * BLK : c * BLK + BLK].astype(jnp.float32).T
                t = t * m.astype(jnp.float32)
                rows, cols = slice(h * BLK, h * BLK + BLK), slice(c * BLK, c * BLK + BLK)
                dst[rows, cols] = (paths[rows, cols] * t).astype(jnp.bfloat16)

    def near(p, o):
        compute(p, o, obuf.at[o, p])
        send(("OD", p, o), obuf.at[o, p], out_ref.at[yh, p], y_to[o - 1])

    def far(p):
        compute(p, 3, obuf.at[3, p])
        for d in range(2):
            send(("OL1", p, d), obuf.at[3, p, half[d]], orel.at[p, d], y_to[d])

    def out_relay(p):
        for d in range(2):
            arrive("OL1", p, d)
            send(("OL2", p, d), orel.at[p, d], out_ref.at[ys[(3, 1)[d]], p, half[d]], y_to[d])

    send(("SP",), s_ref, sbuf.at[yh, core, z, yl], pair)
    r_legs(0)
    r_own(0)
    r_own(1)
    t_start(0)
    own_s.wait()
    arrive("SP")
    for d in range(2):
        mine = sbuf.at[yh, core, z]
        send(("S2", d), mine, mine, y_to[d])
    z_send(0, 0)
    r_direct(0)
    r_legs(1)
    r_onward(0, 0)
    r_relay(0)
    r_onward(0, 1)
    z_send(0, 1)
    for d in range(2):
        arrive("S2", d)
        part = sbuf.at[block[(2, 1)[d]], core, z, d]
        send(("SF", d), part, part, y_to[d])
    z_send(1, 0)
    z_send(2, 0)
    r_direct(1)
    z_send(0, 2)
    t_relay(0)
    for d in range(2):
        arrive("RY", 0, d)
        r_across(1 + d, 0)
    z_send(0, 3)
    for d in range(2):
        arrive("RL2", 0, d)
    r_across(3, 0)
    z_send(1, 1)
    r_relay(1)
    for d in range(2):
        arrive("SF", d)
    z_send(2, 1)
    z_send(3, 0)
    r_onward(1, 0)
    z_send(1, 2)
    r_onward(2, 0)
    s_share(0)
    z_send(2, 2)
    r_onward(3, 0)
    z_send(1, 3)
    for d in range(2):
        arrive("RY", 1, d)
        r_across(1 + d, 1)
    z_send(2, 3)
    z_send(3, 1)
    s_share(1)
    for c in own_r + masks:
        c.wait()
    r_ready(0)
    for d in range(2):
        arrive("RL2", 1, d)
    r_across(3, 1)
    t_done(0)
    z_send(3, 2)
    s_share(2)
    s_ready(1)
    near(0, 1)
    t_start(1)
    r_onward(1, 1)
    s_ready(2)
    near(0, 2)
    z_send(3, 3)
    r_onward(2, 1)
    r_onward(3, 1)
    s_share(3)
    t_relay(1)
    s_ready(0)
    r_ready(1)
    near(1, 1)
    near(1, 2)
    s_ready(3)
    t_done(1)
    far(0)
    far(1)
    out_relay(0)
    out_relay(1)
    for p in range(PASSES):
        compute(p, 0, out_ref.at[yh, p])
    for p in range(PASSES):
        for d in range(2):
            arrive("OD", p, 1 + d)
            arrive("OL2", p, d)
    for copy in sent.values():
        copy.wait_send()


def body(r_vals, s_vals, t_vals, r_pattern, s_pattern, t_pattern):
    any_space = pl.BlockSpec(memory_space=pl.ANY)
    bf16 = jnp.bfloat16
    out = pl.pallas_call(
        kernel,
        out_shape=jax.ShapeDtypeStruct((4, PASSES, H, 256), bf16),
        in_specs=[any_space] * 6,
        out_specs=pl.BlockSpec(memory_space=pltpu.VMEM),
        scratch_shapes=[
            pltpu.VMEM((16, PASSES, H, BLK), bf16),
            pltpu.VMEM((PASSES, 2, H // 2, BLK), bf16),
            pltpu.VMEM((4, 2, 8, 2, 64, 256), bf16),
            pltpu.VMEM((2, 4, 2, 256, BLK), bf16),
            pltpu.VMEM((2, 2, 2, 128, BLK), bf16),
            pltpu.VMEM((4, PASSES, H, 256), bf16),
            pltpu.VMEM((PASSES, 2, H // 2, 256), bf16),
            pltpu.VMEM((PASSES, H, 2048), bf16),
            pltpu.VMEM((4, 2048, 256), bf16),
            pltpu.SMEM((16, 16), jnp.int32),
            pltpu.SMEM((16, 32), jnp.int32),
            pltpu.SMEM((32, 128), jnp.int32),
            pltpu.SemaphoreType.DMA((SEMS,)),
            pltpu.SemaphoreType.DMA((SEMS,)),
            pltpu.SemaphoreType.DMA((8,)),
        ],
        compiler_params=pltpu.CompilerParams(
            collective_id=0, has_side_effects=True, vmem_limit_bytes=48 << 20
        ),
    )(
        r_vals.reshape(4, PASSES, H, BLK),
        s_vals,
        t_vals.reshape(2, 2, 4, 256, BLK),
        r_pattern,
        s_pattern,
        t_pattern,
    )
    return out.reshape(2048, 256)


def solution(mesh):
    placed = (P("row", "col"), P("row", "col"), P(None, ("row", "col")), P(), P(), P())
    return jax.shard_map(
        body, mesh=mesh, in_specs=placed, out_specs=P("row", "col"), check_vma=False
    )
```

```python
import jax
import jax.numpy as jnp
from jax import lax
from jax.experimental import pallas as pl
from jax.experimental.pallas import tpu as pltpu
from jax.sharding import PartitionSpec as P

MESH = pl.DeviceIdType.MESH
BLK = 128
PASSES = 2
H = 512 // PASSES
UNITS = {0: (2,), 1: (0, 1), 2: (0, 1), 3: (0, 1)}
ORDER = (
    ("SU", 1, 1, 1), ("SU", 1, 1, 0), ("TL1", 0, 0), ("SU", 2, 0, 1), ("RX", 0, 0, 1),
    ("SU", 2, 1, 1), ("TD", 0, 0), ("RX", 0, 1, 0), ("SU", 1, 0, 0), ("SU", 2, 1, 0),
    ("SU", 2, 0, 0), ("SU", 1, 0, 1), ("RL1", 0, 0), ("TL1", 0, 1), ("RL1", 0, 1), ("RY", 0, 1),
    ("RY", 0, 0), ("RL1", 1, 0), ("TD", 0, 1), ("Z", 2, 1, 0, 1), ("RX", 0, 0, 0),
    ("Z", 2, 1, 0, 0), ("RF", 0, 0, 1), ("Z", 1, 0, 0, 1), ("TL2", 0, 1), ("SU", 3, 1, 1),
    ("RL1", 1, 1), ("Z", 1, 0, 0, 0), ("SU", 3, 0, 1), ("Z", 1, 1, 0, 1), ("Z", 1, 1, 0, 0),
    ("TL1", 1, 0), ("TL2", 0, 0), ("Z", 2, 0, 0, 1), ("RL2", 0, 1), ("Z", 2, 0, 0, 0),
    ("Z", 2, 1, 1, 0), ("Z", 2, 1, 1, 1), ("RX", 0, 1, 1), ("RL2", 0, 0), ("SU", 3, 0, 0),
    ("Z", 1, 0, 1, 1), ("Z", 1, 0, 1, 0), ("RF", 0, 1, 0), ("RY", 1, 0), ("RX", 2, 0, 0),
    ("RX", 2, 0, 1), ("RY", 1, 1), ("RF", 0, 0, 0), ("RX", 1, 0, 0), ("SU", 3, 1, 0),
    ("Z", 1, 1, 1, 1), ("Z", 2, 0, 1, 1), ("Z", 2, 0, 1, 0), ("TL1", 1, 1), ("Z", 1, 1, 1, 0),
    ("RL2", 1, 0), ("Z", 2, 1, 2, 0), ("Z", 2, 1, 2, 1), ("RX", 1, 0, 1), ("TL2", 1, 0),
    ("Z", 1, 0, 2, 1), ("Z", 1, 0, 2, 0), ("Z", 3, 1, 0, 0), ("SU", 0, 0, 0), ("Z", 3, 1, 0, 1),
    ("RX", 3, 0, 0), ("RX", 3, 0, 1), ("Z", 1, 1, 2, 1), ("SU", 0, 0, 1), ("RL2", 1, 1),
    ("Z", 2, 0, 2, 0), ("Z", 1, 1, 2, 0), ("Z", 2, 0, 2, 1), ("Z", 2, 1, 3, 0), ("Z", 1, 0, 3, 1),
    ("RF", 2, 0, 1), ("RF", 1, 0, 0), ("RF", 2, 0, 0), ("Z", 1, 0, 3, 0), ("Z", 2, 1, 3, 1),
    ("RF", 1, 0, 1), ("RX", 2, 1, 0), ("RX", 2, 1, 1), ("Z", 3, 0, 0, 1), ("Z", 3, 0, 0, 0),
    ("RF", 3, 0, 1), ("RF", 3, 0, 0), ("Z", 1, 1, 3, 1), ("Z", 2, 0, 3, 1), ("Z", 2, 0, 3, 0),
    ("Z", 3, 1, 1, 0), ("RX", 1, 1, 1), ("RX", 1, 1, 0), ("Z", 0, 2, 0, 1), ("SC", 2, 1),
    ("RX", 3, 1, 1), ("RX", 3, 1, 0), ("TL2", 1, 1), ("Z", 1, 1, 3, 0), ("RF", 0, 1, 1),
    ("SC", 1, 0), ("Z", 3, 1, 1, 1), ("RF", 2, 1, 0), ("Z", 3, 0, 1, 0), ("Z", 3, 0, 1, 1),
    ("RF", 2, 1, 1), ("SR", 2, 1), ("Z", 0, 2, 0, 0), ("RR", 0), ("SC", 2, 0), ("SR", 1, 0),
    ("C", 0, 1, 0), ("OD", 0, 1, 0), ("C", 0, 2, 1), ("RF", 1, 1, 1), ("OD", 0, 2, 1),
    ("Z", 3, 1, 2, 0), ("RF", 1, 1, 0), ("SC", 1, 1), ("Z", 3, 1, 2, 1), ("RF", 3, 1, 0),
    ("RF", 3, 1, 1), ("SR", 2, 0), ("Z", 3, 0, 2, 1), ("Z", 3, 0, 2, 0), ("TD", 1, 0), ("SR", 1, 1),
    ("C", 0, 1, 1), ("C", 0, 2, 0), ("OD", 0, 1, 1), ("OD", 0, 2, 0), ("Z", 3, 1, 3, 0),
    ("TD", 1, 1), ("Z", 3, 1, 3, 1), ("RR", 1), ("Z", 3, 0, 3, 1), ("Z", 3, 0, 3, 0),
    ("C", 1, 2, 0), ("OD", 1, 2, 0), ("C", 1, 1, 1), ("OD", 1, 1, 1), ("C", 1, 2, 1),
    ("Z", 0, 2, 1, 1), ("C", 1, 1, 0), ("SC", 3, 1), ("OD", 1, 2, 1), ("OD", 1, 1, 0), ("SC", 3, 0),
    ("SR", 3, 1), ("Z", 0, 2, 1, 0), ("C", 0, 3, 1), ("C", 1, 3, 1), ("Z", 0, 2, 2, 1),
    ("SR", 3, 0), ("C", 1, 3, 0), ("OL1", 1, 0), ("C", 0, 3, 0), ("OL1", 0, 1), ("OL1", 1, 1),
    ("OL1", 0, 0), ("Z", 0, 2, 2, 0), ("Z", 0, 2, 3, 1), ("OL2", 0, 1), ("OL2", 1, 0),
    ("Z", 0, 2, 3, 0), ("OL2", 1, 1), ("OL2", 0, 0), ("SC", 0, 2), ("SR", 0, 2), ("C", 0, 0, 2),
    ("C", 1, 0, 2),
)


def kernel(
    r_ref, s_ref, t_ref, rp_ref, sp_ref, tp_ref, out_ref,
    rbuf, rrel, sbuf, tbuf, trel, obuf, orel, reff, seff, rp, sp, tp, ssem, rsem, usem, lsem,
):
    row, col = lax.axis_index("row"), lax.axis_index("col")
    z, yl, core = lax.div(row, 4), lax.rem(lax.div(row, 2), 2), lax.rem(row, 2)
    yh, x = lax.div(col, 4), lax.rem(col, 4)
    xs = [lax.rem(x + d, 4) for d in range(4)]
    ys = [lax.rem(yh + d, 4) for d in range(4)]
    zs = [lax.rem(z + d, 8) for d in range(8)]
    low = yl * 2 + core
    x_to = [(row, yh * 4 + xs[1]), (row, yh * 4 + xs[3])]
    y_to = [(row, ys[1] * 4 + x), (row, ys[3] * 4 + x)]
    z_to = [(zs[1] * 4 + low, col), (zs[7] * 4 + low, col)]
    pair = (z * 4 + (1 - yl) * 2 + core, col)
    twin = (row + 1 - 2 * core, col)
    s_to = {
        (o, q): (z * 4 + q * 2 + core, ys[d] * 4 + x) for o, d in ((1, 3), (2, 1), (3, 2)) for q in range(2)
    }
    par = lax.rem(yh, 2)
    pars = [1 - par, par]
    block = [yh, ys[1], ys[3], ys[2]]
    half = [pl.ds(0, H // 2), pl.ds(H // 2, H // 2)]

    sent, seen, local = {}, set(), {}

    def send(name, src, dst, device, arrival=None):
        n = len(sent)
        sent[name] = pltpu.make_async_remote_copy(
            src_ref=src, dst_ref=dst, send_sem=ssem.at[n],
            recv_sem=rsem.at[n] if arrival is None else usem.at[arrival],
            device_id=device, device_id_type=MESH,
        )
        sent[name].start()

    def need(*name):
        if name not in seen:
            seen.add(name)
            sent[name].wait_recv()

    def here(name):
        if name not in seen:
            seen.add(name)
            local[name].wait()

    def fetch(name, src, dst):
        local[name] = pltpu.make_async_copy(src, dst, lsem.at[len(local)])
        local[name].start()

    def cols(u):
        return slice(0, 256) if u == 2 else slice(u * BLK, u * BLK + BLK)

    def halves(u):
        return (0, 1) if u == 2 else (u,)

    def SU(o, q, c):
        src, dst = s_ref.at[:, cols(c)], sbuf.at[yh, c, core, z, yl]
        if o:
            send(("SU", o, q, c), src, dst, s_to[o, q], (o * 2 + yl) * 2 + c)
        else:
            send(("SU", o, q, c), src, dst, pair, c)

    def s_came(o, c):
        for q in range(2 if o else 1):
            if ("SU", o, q, c) in seen:
                continue
            seen.add(("SU", o, q, c))
            part = sbuf.at[block[o], c, core, z, q]
            pltpu.make_async_remote_copy(
                src_ref=part, dst_ref=part, send_sem=ssem.at[0], recv_sem=usem.at[(o * 2 + q) * 2 + c],
                device_id=pair, device_id_type=MESH,
            ).wait_recv()

    def Z(o, u, s, d):
        if s:
            need("Z", o, u, s - 1, d)
        else:
            for c in halves(u):
                s_came(o, c)
                if o == 0:
                    here(("S", c))
        part = sbuf.at[block[o], slice(0, 2) if u == 2 else u, core, zs[(-s, s)[d]]]
        if s == 3:
            part = part.at[:, d] if u == 2 else part.at[d]
        send(("Z", o, u, s, d), part, part, z_to[d])

    def SC(o, u):
        for d in range(2):
            for s in range(4):
                need("Z", o, u, s, d)
        part = sbuf.at[block[o], slice(0, 2) if u == 2 else u, core]
        send(("SC", o, u), part, part, twin)

    def SR(o, u):
        need("SC", o, u)
        here(("M", 1))
        j = (block[o] * 4 + x) * 2
        for k in range(16):
            for c in halves(u):
                m = jnp.full((64, BLK), sp[k, j + c].astype(jnp.float32)).astype(jnp.bfloat16)
                for b in range(2):
                    rows = slice(k * 128 + b * 64, k * 128 + b * 64 + 64)
                    seff[o, rows, cols(c)] = sbuf[block[o], c, b, k // 2, k % 2] * m

    def RL1(p, d):
        send(("RL1", p, d), r_ref.at[ys[2], p, half[d]], rrel.at[p, d], y_to[d])

    def RY(p, d):
        send(("RY", p, d), r_ref.at[ys[(1, 3)[d]], p], rbuf.at[col, p], y_to[d])

    def RL2(p, d):
        need("RL1", p, d)
        send(("RL2", p, d), rrel.at[p, d], rbuf.at[ys[(3, 1)[d]] * 4 + x, p, half[d]], y_to[d])

    def RX(j, p, d):
        part = rbuf.at[ys[(0, 3, 1, 2)[j]] * 4 + x, p]
        if j == 0:
            send(("RX", j, p, d), r_ref.at[yh, p], part, x_to[d])
            return
        if j == 3:
            need("RL2", p, 0)
            need("RL2", p, 1)
        else:
            need("RY", p, j - 1)
        send(("RX", j, p, d), part, part, x_to[d])

    def RF(j, p, d):
        need("RX", j, p, d)
        part = rbuf.at[ys[(0, 3, 1, 2)[j]] * 4 + xs[(3, 1)[d]], p, half[d]]
        send(("RF", j, p, d), part, part, x_to[d])

    def RR(p):
        here(("R", p))
        here(("M", 0))
        for d in range(2):
            need("RY", p, d)
            need("RL2", p, d)
            for j in range(4):
                need("RX", j, p, d)
                need("RF", j, p, d)
        for q in range(H // BLK):
            rows = slice(q * BLK, q * BLK + BLK)
            for k in range(16):
                m = rp[k, lax.rem(row, 8) * 16 + yh * 4 + p * (H // BLK) + q].astype(jnp.float32)
                m = jnp.full((BLK, BLK), m).astype(jnp.bfloat16)
                reff[p, rows, k * BLK : k * BLK + BLK] = rbuf[k, p, rows] * m

    def TL1(ph, d):
        rows = pl.ds(d * BLK, BLK)
        send(("TL1", ph, d), t_ref.at[:, pars[ph], xs[2], rows], trel.at[ph, d], x_to[d])

    def TD(ph, d):
        send(("TD", ph, d), t_ref.at[:, pars[ph], xs[(1, 3)[d]]], tbuf.at[ph, x], x_to[d])

    def TL2(ph, d):
        need("TL1", ph, d)
        rows = pl.ds(d * BLK, BLK)
        send(("TL2", ph, d), trel.at[ph, d], tbuf.at[ph, xs[(3, 1)[d]], :, rows], x_to[d])

    def C(p, o, u):
        ph = 1 if o in (0, 3) else 0
        here(("T", ph))
        here(("M", 2))
        for d in range(2):
            need("TD", ph, d)
            need("TL2", ph, d)
        i = lax.div(block[o], 2)
        dst = obuf.at[o, p]
        paths = jnp.dot(reff[p], seff[o, :, cols(u)], preferred_element_type=jnp.float32)
        for h in range(H // BLK):
            q = p * (H // BLK) + h
            for n, c in enumerate(halves(u)):
                m = tp[(block[o] * 4 + x) * 2 + c, lax.rem(row, 8) * 16 + yh * 4 + q]
                t = tbuf[ph, q, i, cols(c)].astype(jnp.float32).T * m.astype(jnp.float32)
                rows = slice(h * BLK, h * BLK + BLK)
                dst[rows, cols(c)] = (paths[rows, cols(n)] * t).astype(jnp.bfloat16)

    def OD(p, o, u):
        send(
            ("OD", p, o, u), obuf.at[o, p, :, cols(u)], out_ref.at[yh, p, :, cols(u)], y_to[o - 1]
        )

    def OL1(p, d):
        send(("OL1", p, d), obuf.at[3, p, half[d]], orel.at[p, d], y_to[d])

    def OL2(p, d):
        need("OL1", p, d)
        send(("OL2", p, d), orel.at[p, d], out_ref.at[ys[(3, 1)[d]], p, half[d]], y_to[d])

    barrier = pltpu.get_barrier_semaphore()
    peers = (*x_to, *z_to, pair, twin, *s_to.values())
    for device in peers:
        pl.semaphore_signal(barrier, inc=1, device_id=device, device_id_type=MESH)
    for c in range(2):
        fetch(("S", c), s_ref.at[:, cols(c)], sbuf.at[yh, c, core, z, yl])
    for p in range(PASSES):
        fetch(("R", p), r_ref.at[yh, p], rbuf.at[col, p])
    for ph in range(2):
        fetch(("T", ph), t_ref.at[:, pars[ph], x], tbuf.at[ph, x])
    lanes = pl.ds(pl.multiple_of(lax.div(row, 8) * BLK, BLK), BLK)
    fetch(("M", 0), rp_ref.at[:, lanes], rp)
    fetch(("M", 1), sp_ref, sp)
    fetch(("M", 2), tp_ref.at[:, lanes], tp)
    pl.semaphore_wait(barrier, len(peers))

    steps = dict(
        SU=SU, Z=Z, SC=SC, SR=SR, RL1=RL1, RY=RY, RL2=RL2, RX=RX, RF=RF, RR=RR,
        TL1=TL1, TD=TD, TL2=TL2, C=C, OD=OD, OL1=OL1, OL2=OL2,
    )
    for step, *where in ORDER:
        steps[step](*where)
    for p in range(PASSES):
        fetch(("O", p), obuf.at[0, p], out_ref.at[yh, p])
    for p in range(PASSES):
        here(("O", p))
    for name in sent:
        if name[0] in ("OD", "OL2"):
            need(*name)
    for copy in sent.values():
        copy.wait_send()


def body(r_vals, s_vals, t_vals, r_pattern, s_pattern, t_pattern):
    hbm = pl.BlockSpec(memory_space=pltpu.HBM)
    bf16 = jnp.bfloat16
    out = pl.pallas_call(
        kernel,
        out_shape=jax.ShapeDtypeStruct((4, PASSES, H, 256), bf16),
        in_specs=[hbm] * 6,
        out_specs=hbm,
        scratch_shapes=[
            pltpu.VMEM((16, PASSES, H, BLK), bf16),
            pltpu.VMEM((PASSES, 2, H // 2, BLK), bf16),
            pltpu.VMEM((4, 2, 2, 8, 2, 64, BLK), bf16),
            pltpu.VMEM((2, 4, 2, 256, BLK), bf16),
            pltpu.VMEM((2, 2, 2, BLK, BLK), bf16),
            pltpu.VMEM((4, PASSES, H, 256), bf16),
            pltpu.VMEM((PASSES, 2, H // 2, 256), bf16),
            pltpu.VMEM((PASSES, H, 2048), bf16),
            pltpu.VMEM((4, 2048, 256), bf16),
            pltpu.SMEM((16, BLK), jnp.int32),
            pltpu.SMEM((16, 32), jnp.int32),
            pltpu.SMEM((32, BLK), jnp.int32),
            pltpu.SemaphoreType.DMA((len(ORDER),)),
            pltpu.SemaphoreType.DMA((len(ORDER),)),
            pltpu.SemaphoreType.DMA((16,)),
            pltpu.SemaphoreType.DMA((9 + PASSES,)),
        ],
        compiler_params=pltpu.CompilerParams(
            collective_id=0, has_side_effects=True, vmem_limit_bytes=67043328
        ),
    )(
        r_vals.reshape(4, PASSES, H, BLK),
        s_vals,
        t_vals.reshape(2, 2, 4, 256, BLK),
        r_pattern.T,
        s_pattern,
        t_pattern,
    )
    return out.reshape(2048, 256)


def solution(mesh):
    placed = (P("row", "col"), P("row", "col"), P(None, ("row", "col")), P(), P(), P())
    return jax.shard_map(
        body, mesh=mesh, in_specs=placed, out_specs=P("row", "col"), check_vma=False
    )
```

```python
import jax
import jax.numpy as jnp
from jax import lax
from jax.experimental import pallas as pl
from jax.experimental.pallas import tpu as pltpu
from jax.sharding import PartitionSpec as P

MESH = pl.DeviceIdType.MESH
BLK = 128
PASSES = 2
H = 512 // PASSES
UNITS = {0: (2,), 1: (0, 1), 2: (0, 1), 3: (0, 1)}
ORDER = (
    ("SU", 1, 0, 0), ("SU", 2, 1, 1), ("TL1", 0, 0), ("TL1", 0, 1), ("SU", 1, 0, 1),
    ("SU", 2, 0, 1), ("RX", 0, 1, 0), ("RX", 0, 1, 1), ("SU", 1, 1, 1), ("RL1", 0, 0),
    ("SU", 1, 1, 0), ("RX", 0, 0, 0), ("RX", 0, 0, 1), ("SU", 2, 1, 0), ("RL1", 0, 1),
    ("SU", 2, 0, 0), ("TL2", 0, 1), ("TL1", 1, 0), ("RY", 0, 0), ("RY", 0, 1), ("Z", 2, 1, 0, 0),
    ("Z", 2, 1, 0, 1), ("RF", 0, 1, 1), ("RF", 0, 1, 0), ("Z", 1, 1, 0, 0), ("Z", 1, 1, 0, 1),
    ("TL2", 0, 0), ("TD", 0, 1), ("Z", 1, 0, 0, 0), ("Z", 1, 0, 0, 1), ("RL1", 1, 0), ("RY", 1, 1),
    ("RF", 0, 0, 0), ("Z", 2, 0, 0, 0), ("Z", 2, 0, 0, 1), ("TD", 0, 0), ("Z", 2, 1, 1, 0),
    ("Z", 2, 1, 1, 1), ("RL2", 0, 0), ("RF", 0, 0, 1), ("Z", 1, 1, 1, 0), ("Z", 1, 1, 1, 1),
    ("Z", 1, 0, 1, 0), ("Z", 1, 0, 1, 1), ("RL2", 0, 1), ("SU", 3, 0, 0), ("RX", 2, 0, 1),
    ("SU", 0, 0, 0), ("Z", 2, 0, 1, 0), ("Z", 2, 0, 1, 1), ("SU", 3, 0, 1), ("SU", 0, 0, 1),
    ("RX", 1, 0, 0), ("RL1", 1, 1), ("Z", 2, 1, 2, 0), ("Z", 2, 1, 2, 1), ("RX", 1, 0, 1),
    ("RL2", 1, 0), ("SU", 3, 1, 0), ("Z", 1, 1, 2, 0), ("Z", 1, 1, 2, 1), ("RX", 2, 0, 0),
    ("Z", 1, 0, 2, 0), ("Z", 1, 0, 2, 1), ("RX", 2, 1, 1), ("RY", 1, 0), ("SU", 3, 1, 1),
    ("Z", 0, 2, 0, 0), ("Z", 0, 2, 0, 1), ("RH", 0, 0, 0), ("RX", 2, 1, 0), ("RH", 0, 0, 1),
    ("Z", 2, 0, 2, 1), ("Z", 2, 1, 3, 0), ("RH", 1, 0, 1), ("Z", 2, 0, 2, 0), ("Z", 2, 1, 3, 1),
    ("RH", 1, 0, 0), ("RF", 2, 0, 1), ("RL2", 1, 1), ("Z", 1, 1, 3, 0), ("Z", 1, 1, 3, 1),
    ("Z", 1, 0, 3, 0), ("Z", 1, 0, 3, 1), ("RF", 1, 0, 0), ("RF", 1, 0, 1), ("Z", 3, 0, 0, 0),
    ("Z", 3, 0, 0, 1), ("RF", 3, 0, 0), ("RH", 0, 1, 1), ("Z", 0, 2, 1, 0), ("Z", 0, 2, 1, 1),
    ("RH", 0, 1, 0), ("RF", 2, 1, 1), ("RF", 2, 0, 0), ("RF", 3, 0, 1), ("SC", 2, 1),
    ("Z", 2, 0, 3, 0), ("Z", 2, 0, 3, 1), ("RF", 2, 1, 0), ("SC", 1, 1), ("Z", 3, 1, 0, 0),
    ("Z", 3, 1, 0, 1), ("RX", 1, 1, 1), ("RX", 1, 1, 0), ("SC", 1, 0), ("Z", 3, 0, 1, 0),
    ("Z", 3, 0, 1, 1), ("RH", 1, 1, 1), ("SR", 2, 1), ("RH", 1, 1, 0), ("Z", 0, 2, 2, 0),
    ("Z", 0, 2, 2, 1), ("TL1", 1, 1), ("RR", 0), ("SC", 2, 0), ("C", 0, 2, 1), ("SR", 1, 1),
    ("OD", 0, 2, 1), ("C", 0, 1, 1), ("RF", 3, 1, 0), ("OD", 0, 1, 1), ("Z", 3, 1, 1, 0),
    ("Z", 3, 1, 1, 1), ("RF", 1, 1, 1), ("Z", 3, 0, 2, 0), ("Z", 3, 0, 2, 1), ("RF", 1, 1, 0),
    ("RF", 3, 1, 1), ("SR", 2, 0), ("SR", 1, 0), ("TL2", 1, 0), ("C", 0, 1, 0), ("TD", 1, 1),
    ("C", 0, 2, 0), ("OD", 0, 2, 0), ("OD", 0, 1, 0), ("Z", 0, 2, 3, 0), ("Z", 0, 2, 3, 1),
    ("TD", 1, 0), ("Z", 3, 1, 2, 0), ("Z", 3, 1, 2, 1), ("Z", 3, 0, 3, 0), ("Z", 3, 0, 3, 1),
    ("RR", 1), ("C", 1, 1, 1), ("TL2", 1, 1), ("C", 1, 2, 1), ("C", 1, 1, 0), ("OD", 1, 2, 1),
    ("OD", 1, 1, 1), ("C", 1, 2, 0), ("Z", 3, 1, 3, 0), ("Z", 3, 1, 3, 1), ("SC", 3, 0),
    ("OD", 1, 2, 0), ("OD", 1, 1, 0), ("SC", 0, 2), ("SR", 3, 0), ("C", 0, 3, 0), ("C", 1, 3, 0),
    ("SC", 3, 1), ("OL1", 0, 1, 0), ("OL1", 0, 0, 0), ("OL1", 1, 1, 0), ("OL1", 1, 0, 0),
    ("SR", 0, 2), ("C", 0, 0, 2), ("C", 1, 0, 2), ("SR", 3, 1), ("C", 0, 3, 1), ("C", 1, 3, 1),
    ("OL1", 0, 0, 1), ("OL1", 0, 1, 1), ("OL1", 1, 0, 1), ("OL1", 1, 1, 1), ("OL2", 0, 0, 0),
    ("OL2", 0, 1, 0), ("OL2", 1, 0, 0), ("OL2", 1, 1, 0), ("OL2", 0, 0, 1), ("OL2", 0, 1, 1),
    ("OL2", 1, 0, 1), ("OL2", 1, 1, 1),
)


def kernel(
    r_ref, s_ref, t_ref, rp_ref, sp_ref, tp_ref, out_ref,
    rbuf, rrel, sbuf, tbuf, trel, obuf, orel, reff, seff, rp, sp, tp, ssem, rsem, usem, lsem,
):
    row, col = lax.axis_index("row"), lax.axis_index("col")
    z, yl, core = lax.div(row, 4), lax.rem(lax.div(row, 2), 2), lax.rem(row, 2)
    yh, x = lax.div(col, 4), lax.rem(col, 4)
    xs = [lax.rem(x + d, 4) for d in range(4)]
    ys = [lax.rem(yh + d, 4) for d in range(4)]
    zs = [lax.rem(z + d, 8) for d in range(8)]
    low = yl * 2 + core
    x_to = [(row, yh * 4 + xs[1]), (row, yh * 4 + xs[3])]
    y_to = [(row, ys[1] * 4 + x), (row, ys[3] * 4 + x)]
    z_to = [(zs[1] * 4 + low, col), (zs[7] * 4 + low, col)]
    pair = (z * 4 + (1 - yl) * 2 + core, col)
    twin = (row + 1 - 2 * core, col)
    s_to = {
        (o, q): (z * 4 + q * 2 + core, ys[d] * 4 + x) for o, d in ((1, 3), (2, 1), (3, 2)) for q in range(2)
    }
    par = lax.rem(yh, 2)
    pars = [1 - par, par]
    block = [yh, ys[1], ys[3], ys[2]]
    half = [pl.ds(0, H // 2), pl.ds(H // 2, H // 2)]

    sent, seen, local = {}, set(), {}

    def send(name, src, dst, device, arrival=None):
        n = len(sent)
        sent[name] = pltpu.make_async_remote_copy(
            src_ref=src, dst_ref=dst, send_sem=ssem.at[n],
            recv_sem=rsem.at[n] if arrival is None else usem.at[arrival],
            device_id=device, device_id_type=MESH,
        )
        sent[name].start()

    def need(*name):
        if name not in seen:
            seen.add(name)
            sent[name].wait_recv()

    def here(name):
        if name not in seen:
            seen.add(name)
            local[name].wait()

    def fetch(name, src, dst):
        local[name] = pltpu.make_async_copy(src, dst, lsem.at[len(local)])
        local[name].start()

    def cols(u):
        return slice(0, 256) if u == 2 else slice(u * BLK, u * BLK + BLK)

    def halves(u):
        return (0, 1) if u == 2 else (u,)

    def SU(o, q, c):
        src, dst = s_ref.at[:, cols(c)], sbuf.at[yh, c, core, z, yl]
        if o:
            send(("SU", o, q, c), src, dst, s_to[o, q], (o * 2 + yl) * 2 + c)
        else:
            send(("SU", o, q, c), src, dst, pair, c)

    def s_came(o, c):
        for q in range(2 if o else 1):
            if ("SU", o, q, c) in seen:
                continue
            seen.add(("SU", o, q, c))
            part = sbuf.at[block[o], c, core, z, q]
            pltpu.make_async_remote_copy(
                src_ref=part, dst_ref=part, send_sem=ssem.at[0], recv_sem=usem.at[(o * 2 + q) * 2 + c],
                device_id=pair, device_id_type=MESH,
            ).wait_recv()

    def Z(o, u, s, d):
        if s:
            need("Z", o, u, s - 1, d)
        else:
            for c in halves(u):
                s_came(o, c)
                if o == 0:
                    here(("S", c))
        part = sbuf.at[block[o], slice(0, 2) if u == 2 else u, core, zs[(-s, s)[d]]]
        if s == 3:
            part = part.at[:, d] if u == 2 else part.at[d]
        send(("Z", o, u, s, d), part, part, z_to[d])

    def SC(o, u):
        for d in range(2):
            for s in range(4):
                need("Z", o, u, s, d)
        part = sbuf.at[block[o], slice(0, 2) if u == 2 else u, core]
        send(("SC", o, u), part, part, twin)

    def SR(o, u):
        need("SC", o, u)
        here(("M", 1))
        j = (block[o] * 4 + x) * 2
        for k in range(16):
            for c in halves(u):
                m = jnp.full((64, BLK), sp[k, j + c].astype(jnp.float32)).astype(jnp.bfloat16)
                for b in range(2):
                    rows = slice(k * 128 + b * 64, k * 128 + b * 64 + 64)
                    seff[o, rows, cols(c)] = sbuf[block[o], c, b, k // 2, k % 2] * m

    def RL1(p, d):
        send(("RL1", p, d), r_ref.at[ys[2], p, half[d]], rrel.at[p, d], y_to[d])

    def RY(p, d):
        send(("RY", p, d), r_ref.at[ys[(1, 3)[d]], p], rbuf.at[col, p], y_to[d])

    def RL2(p, d):
        need("RL1", p, d)
        send(("RL2", p, d), rrel.at[p, d], rbuf.at[ys[(3, 1)[d]] * 4 + x, p, half[d]], y_to[d])

    def RX(j, p, d):
        part = rbuf.at[ys[(0, 3, 1, 2)[j]] * 4 + x, p]
        if j == 0:
            send(("RX", j, p, d), r_ref.at[yh, p], part, x_to[d])
            return
        need("RY", p, j - 1)
        send(("RX", j, p, d), part, part, x_to[d])

    def RH(h, p, d):
        need("RL2", p, h)
        part = rbuf.at[ys[2] * 4 + x, p, half[h]]
        send(("RH", h, p, d), part, part, x_to[d])

    def RF(j, p, d):
        if j == 3:
            need("RH", d, p, d)
        else:
            need("RX", j, p, d)
        part = rbuf.at[ys[(0, 3, 1, 2)[j]] * 4 + xs[(3, 1)[d]], p, half[d]]
        send(("RF", j, p, d), part, part, x_to[d])

    def RR(p):
        here(("R", p))
        here(("M", 0))
        for d in range(2):
            need("RY", p, d)
            need("RL2", p, d)
            for j in range(4):
                if j < 3:
                    need("RX", j, p, d)
                need("RF", j, p, d)
            for h in range(2):
                need("RH", h, p, d)
        for q in range(H // BLK):
            rows = slice(q * BLK, q * BLK + BLK)
            for k in range(16):
                m = rp[k, lax.rem(row, 8) * 16 + yh * 4 + p * (H // BLK) + q].astype(jnp.float32)
                m = jnp.full((BLK, BLK), m).astype(jnp.bfloat16)
                reff[p, rows, k * BLK : k * BLK + BLK] = rbuf[k, p, rows] * m

    def TL1(ph, d):
        rows = pl.ds(d * BLK, BLK)
        send(("TL1", ph, d), t_ref.at[:, pars[ph], xs[2], rows], trel.at[ph, d], x_to[d])

    def TD(ph, d):
        send(("TD", ph, d), t_ref.at[:, pars[ph], xs[(1, 3)[d]]], tbuf.at[ph, x], x_to[d])

    def TL2(ph, d):
        need("TL1", ph, d)
        rows = pl.ds(d * BLK, BLK)
        send(("TL2", ph, d), trel.at[ph, d], tbuf.at[ph, xs[(3, 1)[d]], :, rows], x_to[d])

    def C(p, o, u):
        ph = 1 if o in (0, 3) else 0
        here(("T", ph))
        here(("M", 2))
        for d in range(2):
            need("TD", ph, d)
            need("TL2", ph, d)
        i = lax.div(block[o], 2)
        dst = obuf.at[o, p] if o else out_ref.at[yh, p]
        paths = jnp.dot(reff[p], seff[o, :, cols(u)], preferred_element_type=jnp.float32)
        for h in range(H // BLK):
            q = p * (H // BLK) + h
            for n, c in enumerate(halves(u)):
                m = tp[(block[o] * 4 + x) * 2 + c, lax.rem(row, 8) * 16 + yh * 4 + q]
                t = tbuf[ph, q, i, cols(c)].astype(jnp.float32).T * m.astype(jnp.float32)
                rows = slice(h * BLK, h * BLK + BLK)
                dst[rows, cols(c)] = (paths[rows, cols(n)] * t).astype(jnp.bfloat16)

    def OD(p, o, u):
        send(
            ("OD", p, o, u), obuf.at[o, p, :, cols(u)], out_ref.at[yh, p, :, cols(u)], y_to[o - 1]
        )

    def OL1(p, d, u):
        part = obuf.at[3, p, half[d], cols(u)]
        send(("OL1", p, d, u), part, orel.at[p, d, :, cols(u)], y_to[d])

    def OL2(p, d, u):
        need("OL1", p, d, u)
        dst = out_ref.at[ys[(3, 1)[d]], p, half[d], cols(u)]
        send(("OL2", p, d, u), orel.at[p, d, :, cols(u)], dst, y_to[d])

    barrier = pltpu.get_barrier_semaphore()
    peers = (*x_to, *z_to, pair, twin, *s_to.values())
    for device in peers:
        pl.semaphore_signal(barrier, inc=1, device_id=device, device_id_type=MESH)
    for c in range(2):
        fetch(("S", c), s_ref.at[:, cols(c)], sbuf.at[yh, c, core, z, yl])
    for p in range(PASSES):
        fetch(("R", p), r_ref.at[yh, p], rbuf.at[col, p])
    for ph in range(2):
        fetch(("T", ph), t_ref.at[:, pars[ph], x], tbuf.at[ph, x])
    lanes = pl.ds(pl.multiple_of(lax.div(row, 8) * BLK, BLK), BLK)
    fetch(("M", 0), rp_ref.at[:, lanes], rp)
    fetch(("M", 1), sp_ref, sp)
    fetch(("M", 2), tp_ref.at[:, lanes], tp)
    pl.semaphore_wait(barrier, len(peers))

    steps = dict(
        SU=SU, Z=Z, SC=SC, SR=SR, RL1=RL1, RY=RY, RL2=RL2, RX=RX, RH=RH, RF=RF, RR=RR,
        TL1=TL1, TD=TD, TL2=TL2, C=C, OD=OD, OL1=OL1, OL2=OL2,
    )
    for step, *where in ORDER:
        steps[step](*where)
    for name in sent:
        if name[0] in ("OD", "OL2"):
            need(*name)
    for copy in sent.values():
        copy.wait_send()


def body(r_vals, s_vals, t_vals, r_pattern, s_pattern, t_pattern):
    hbm = pl.BlockSpec(memory_space=pltpu.HBM)
    bf16 = jnp.bfloat16
    out = pl.pallas_call(
        kernel,
        out_shape=jax.ShapeDtypeStruct((4, PASSES, H, 256), bf16),
        in_specs=[hbm] * 6,
        out_specs=pl.BlockSpec(memory_space=pltpu.VMEM),
        scratch_shapes=[
            pltpu.VMEM((16, PASSES, H, BLK), bf16),
            pltpu.VMEM((PASSES, 2, H // 2, BLK), bf16),
            pltpu.VMEM((4, 2, 2, 8, 2, 64, BLK), bf16),
            pltpu.VMEM((2, 4, 2, 256, BLK), bf16),
            pltpu.VMEM((2, 2, 2, BLK, BLK), bf16),
            pltpu.VMEM((4, PASSES, H, 256), bf16),
            pltpu.VMEM((PASSES, 2, H // 2, 256), bf16),
            pltpu.VMEM((PASSES, H, 2048), bf16),
            pltpu.VMEM((4, 2048, 256), bf16),
            pltpu.SMEM((16, BLK), jnp.int32),
            pltpu.SMEM((16, 32), jnp.int32),
            pltpu.SMEM((32, BLK), jnp.int32),
            pltpu.SemaphoreType.DMA((len(ORDER),)),
            pltpu.SemaphoreType.DMA((len(ORDER),)),
            pltpu.SemaphoreType.DMA((16,)),
            pltpu.SemaphoreType.DMA((9,)),
        ],
        compiler_params=pltpu.CompilerParams(
            collective_id=0, has_side_effects=True, vmem_limit_bytes=48 << 20
        ),
    )(*[pltpu.with_memory_space_constraint(a, pltpu.HBM) for a in (
        r_vals.reshape(4, PASSES, H, BLK),
        s_vals,
        t_vals.reshape(2, 2, 4, 256, BLK),
        r_pattern.T,
        s_pattern,
        t_pattern,
    )])
    return out.reshape(2048, 256)


def solution(mesh):
    placed = (P("row", "col"), P("row", "col"), P(None, ("row", "col")), P(), P(), P())
    return jax.shard_map(
        body, mesh=mesh, in_specs=placed, out_specs=P("row", "col"), check_vma=False
    )
```

```python
import jax
import jax.numpy as jnp
from jax import lax
from jax.experimental import pallas as pl
from jax.experimental.pallas import tpu as pltpu
from jax.sharding import PartitionSpec as P

MESH = pl.DeviceIdType.MESH
BLK = 128
PASSES = 2
H = 512 // PASSES
UNITS = {0: (2,), 1: (0, 1), 2: (0, 1), 3: (0, 1)}
SKIPS = ((1, 0), (2, 0))
ORDER = (
    ("SU", 1, 0, 0), ("SU", 2, 1, 0), ("SU", 0, 0, 1), ("TD", 0, 0), ("SU", 1, 1, 0), ("RL1", 0, 1),
    ("RX", 0, 0, 1), ("SU", 2, 0, 1), ("SU", 1, 0, 1), ("SU", 2, 0, 0), ("TL1", 0, 1),
    ("SU", 2, 1, 1), ("SU", 1, 1, 1), ("RY", 0, 1), ("RX", 0, 1, 0), ("TD", 0, 1), ("TL1", 0, 0),
    ("RL1", 0, 0), ("SU", 0, 0, 0), ("RY", 0, 0), ("Z", 1, 0, 1, 1), ("Z", 1, 0, 1, 0),
    ("SU", 3, 0, 1), ("Z", 2, 0, 1, 0), ("Z", 2, 0, 1, 1), ("RL2", 0, 1), ("RF", 0, 1, 0),
    ("RL1", 1, 1), ("Z", 2, 1, 0, 0), ("Z", 1, 0, 0, 0), ("RX", 0, 1, 1), ("Z", 2, 1, 0, 1),
    ("RX", 0, 0, 0), ("Z", 1, 1, 0, 1), ("RL2", 0, 0), ("TL2", 0, 0), ("Z", 2, 0, 0, 1),
    ("RF", 0, 0, 1), ("RL1", 1, 0), ("SU", 3, 1, 1), ("TL2", 0, 1), ("Z", 1, 1, 0, 0),
    ("Z", 1, 0, 0, 1), ("SU", 3, 1, 0), ("Z", 1, 0, 3, 0), ("SU", 3, 0, 0), ("Z", 1, 0, 3, 1),
    ("RX", 2, 0, 1), ("Z", 1, 0, 2, 0), ("RX", 1, 0, 0), ("RY", 1, 1), ("RX", 2, 0, 0),
    ("RY", 1, 0), ("Z", 1, 0, 2, 1), ("Z", 2, 1, 1, 0), ("Z", 2, 0, 3, 0), ("Z", 2, 1, 1, 1),
    ("RX", 1, 0, 1), ("Z", 1, 1, 1, 1), ("Z", 2, 0, 3, 1), ("Z", 1, 1, 1, 0), ("RH", 1, 0, 1),
    ("Z", 2, 0, 2, 0), ("TL1", 1, 1), ("Z", 2, 0, 0, 0), ("RH", 0, 0, 0), ("Z", 2, 0, 2, 1),
    ("RH", 0, 0, 1), ("RL2", 1, 1), ("RH", 1, 0, 0), ("Z", 3, 1, 0, 1), ("Z", 3, 1, 0, 0),
    ("SC", 1, 0), ("RF", 0, 0, 0), ("RF", 1, 0, 0), ("RL2", 1, 0), ("RF", 2, 0, 1),
    ("Z", 2, 1, 2, 1), ("Z", 2, 1, 2, 0), ("Z", 1, 1, 2, 1), ("Z", 3, 0, 0, 0), ("Z", 3, 0, 0, 1),
    ("Z", 1, 1, 2, 0), ("Z", 0, 2, 0, 0), ("RF", 1, 0, 1), ("RF", 2, 0, 0), ("RF", 3, 0, 0),
    ("RF", 3, 0, 1), ("Z", 0, 2, 0, 1), ("SR", 1, 0), ("SC", 2, 0), ("RX", 2, 1, 0),
    ("RX", 1, 1, 0), ("RX", 2, 1, 1), ("Z", 2, 1, 3, 1), ("Z", 2, 1, 3, 0), ("Z", 3, 1, 1, 1),
    ("RX", 1, 1, 1), ("Z", 3, 1, 1, 0), ("Z", 1, 1, 3, 1), ("Z", 3, 0, 1, 1), ("RH", 1, 1, 1),
    ("Z", 1, 1, 3, 0), ("SR", 2, 0), ("Z", 3, 0, 1, 0), ("RH", 0, 1, 0), ("RR", 0),
    ("Z", 0, 2, 1, 1), ("Z", 0, 2, 1, 0), ("TL1", 1, 0), ("RF", 0, 1, 1), ("SC", 2, 1),
    ("C", 0, 2, 0), ("RF", 2, 1, 0), ("RF", 2, 1, 1), ("Z", 3, 1, 2, 0), ("C", 0, 1, 0),
    ("Z", 3, 1, 2, 1), ("SC", 1, 1), ("RH", 0, 1, 1), ("RF", 1, 1, 0), ("RF", 1, 1, 1),
    ("Z", 3, 0, 2, 1), ("Z", 3, 0, 2, 0), ("OD", 0, 2, 0), ("OD", 0, 1, 0), ("RF", 3, 1, 0),
    ("RF", 3, 1, 1), ("RH", 1, 1, 0), ("SR", 2, 1), ("C", 0, 2, 1), ("Z", 0, 2, 2, 1),
    ("Z", 0, 2, 2, 0), ("OD", 0, 2, 1), ("TD", 1, 0), ("TD", 1, 1), ("SR", 1, 1), ("Z", 3, 1, 3, 0),
    ("TL2", 1, 0), ("C", 0, 1, 1), ("Z", 3, 1, 3, 1), ("OD", 0, 1, 1), ("Z", 3, 0, 3, 0),
    ("TL2", 1, 1), ("Z", 3, 0, 3, 1), ("RR", 1), ("C", 1, 1, 0), ("OD", 1, 1, 0), ("C", 1, 2, 0),
    ("OD", 1, 2, 0), ("Z", 0, 2, 3, 1), ("Z", 0, 2, 3, 0), ("SC", 3, 1), ("C", 1, 2, 1),
    ("OD", 1, 2, 1), ("C", 1, 1, 1), ("OD", 1, 1, 1), ("SC", 3, 0), ("SR", 3, 1), ("C", 0, 3, 1),
    ("SC", 0, 2), ("OL1", 0, 1, 1), ("SR", 3, 0), ("C", 0, 3, 0), ("C", 1, 3, 1), ("OL1", 0, 0, 0),
    ("OL1", 0, 0, 1), ("OL1", 1, 0, 1), ("OL1", 0, 1, 0), ("SR", 0, 2), ("C", 1, 3, 0),
    ("OL1", 1, 1, 0), ("C", 1, 0, 2), ("OL1", 1, 1, 1), ("OL1", 1, 0, 0), ("OL2", 0, 0, 0),
    ("OL2", 0, 1, 1), ("OL2", 0, 0, 1), ("OL2", 0, 1, 0), ("OL2", 1, 0, 1), ("OL2", 1, 1, 0),
    ("OL2", 1, 0, 0), ("OL2", 1, 1, 1), ("C", 0, 0, 2),
)


def kernel(
    r_ref, s_ref, t_ref, rp_ref, sp_ref, tp_ref, out_ref,
    rbuf, rrel, sbuf, tbuf, trel, obuf, orel, reff, seff, rp, sp, tp, ssem, rsem, usem, lsem,
):
    row, col = lax.axis_index("row"), lax.axis_index("col")
    z, yl, core = lax.div(row, 4), lax.rem(lax.div(row, 2), 2), lax.rem(row, 2)
    yh, x = lax.div(col, 4), lax.rem(col, 4)
    xs = [lax.rem(x + d, 4) for d in range(4)]
    ys = [lax.rem(yh + d, 4) for d in range(4)]
    zs = [lax.rem(z + d, 8) for d in range(8)]
    low = yl * 2 + core
    x_to = [(row, yh * 4 + xs[1]), (row, yh * 4 + xs[3])]
    y_to = [(row, ys[1] * 4 + x), (row, ys[3] * 4 + x)]
    z_to = [(zs[1] * 4 + low, col), (zs[7] * 4 + low, col)]
    z_skip = [(zs[2] * 4 + low, col), (zs[6] * 4 + low, col)]
    pair = (z * 4 + (1 - yl) * 2 + core, col)
    twin = (row + 1 - 2 * core, col)
    s_to = {
        (o, q): (z * 4 + q * 2 + core, ys[d] * 4 + x) for o, d in ((1, 3), (2, 1), (3, 2)) for q in range(2)
    }
    par = lax.rem(yh, 2)
    pars = [1 - par, par]
    block = [yh, ys[1], ys[3], ys[2]]
    half = [pl.ds(0, H // 2), pl.ds(H // 2, H // 2)]

    sent, seen, local = {}, set(), {}

    def send(name, src, dst, device, arrival=None):
        n = len(sent)
        sent[name] = pltpu.make_async_remote_copy(
            src_ref=src, dst_ref=dst, send_sem=ssem.at[n],
            recv_sem=rsem.at[n] if arrival is None else usem.at[arrival],
            device_id=device, device_id_type=MESH,
        )
        sent[name].start()

    def need(*name):
        if name not in seen:
            seen.add(name)
            sent[name].wait_recv()

    def here(name):
        if name not in seen:
            seen.add(name)
            local[name].wait()

    def fetch(name, src, dst):
        local[name] = pltpu.make_async_copy(src, dst, lsem.at[len(local)])
        local[name].start()

    def cols(u):
        return slice(0, 256) if u == 2 else slice(u * BLK, u * BLK + BLK)

    def halves(u):
        return (0, 1) if u == 2 else (u,)

    def SU(o, q, c):
        src, dst = s_ref.at[:, cols(c)], sbuf.at[yh, c, core, z, yl]
        if o:
            send(("SU", o, q, c), src, dst, s_to[o, q], (o * 2 + yl) * 2 + c)
        else:
            send(("SU", o, q, c), src, dst, pair, c)

    def s_came(o, c):
        for q in range(2 if o else 1):
            if ("SU", o, q, c) in seen:
                continue
            seen.add(("SU", o, q, c))
            part = sbuf.at[block[o], c, core, z, q]
            pltpu.make_async_remote_copy(
                src_ref=part, dst_ref=part, send_sem=ssem.at[0], recv_sem=usem.at[(o * 2 + q) * 2 + c],
                device_id=pair, device_id_type=MESH,
            ).wait_recv()

    def Z(o, u, s, d):
        skip = (o, u) in SKIPS
        back = (0, 0, 2, 2)[s] if skip else s
        if back:
            need("Z", o, u, back - 1, d)
        else:
            for c in halves(u):
                s_came(o, c)
                if o == 0:
                    here(("S", c))
        part = sbuf.at[block[o], slice(0, 2) if u == 2 else u, core, zs[(-back, back)[d]]]
        if s == 3:
            part = part.at[:, d] if u == 2 else part.at[d]
        send(("Z", o, u, s, d), part, part, (z_skip if skip and s in (1, 3) else z_to)[d])

    def SC(o, u):
        for d in range(2):
            for s in range(4):
                need("Z", o, u, s, d)
        part = sbuf.at[block[o], slice(0, 2) if u == 2 else u, core]
        send(("SC", o, u), part, part, twin)

    def SR(o, u):
        need("SC", o, u)
        here(("M", 1))
        j = (block[o] * 4 + x) * 2
        for k in range(16):
            for c in halves(u):
                m = jnp.full((64, BLK), sp[k, j + c].astype(jnp.float32)).astype(jnp.bfloat16)
                for b in range(2):
                    rows = slice(k * 128 + b * 64, k * 128 + b * 64 + 64)
                    seff[o, rows, cols(c)] = sbuf[block[o], c, b, k // 2, k % 2] * m

    def RL1(p, d):
        send(("RL1", p, d), r_ref.at[ys[2], p, half[d]], rrel.at[p, d], y_to[d])

    def RY(p, d):
        send(("RY", p, d), r_ref.at[ys[(1, 3)[d]], p], rbuf.at[col, p], y_to[d])

    def RL2(p, d):
        need("RL1", p, d)
        send(("RL2", p, d), rrel.at[p, d], rbuf.at[ys[(3, 1)[d]] * 4 + x, p, half[d]], y_to[d])

    def RX(j, p, d):
        part = rbuf.at[ys[(0, 3, 1, 2)[j]] * 4 + x, p]
        if j == 0:
            send(("RX", j, p, d), r_ref.at[yh, p], part, x_to[d])
            return
        need("RY", p, j - 1)
        send(("RX", j, p, d), part, part, x_to[d])

    def RH(h, p, d):
        need("RL2", p, h)
        part = rbuf.at[ys[2] * 4 + x, p, half[h]]
        send(("RH", h, p, d), part, part, x_to[d])

    def RF(j, p, d):
        if j == 3:
            need("RH", d, p, d)
        else:
            need("RX", j, p, d)
        part = rbuf.at[ys[(0, 3, 1, 2)[j]] * 4 + xs[(3, 1)[d]], p, half[d]]
        send(("RF", j, p, d), part, part, x_to[d])

    def RR(p):
        here(("R", p))
        here(("M", 0))
        for d in range(2):
            need("RY", p, d)
            need("RL2", p, d)
            for j in range(4):
                if j < 3:
                    need("RX", j, p, d)
                need("RF", j, p, d)
            for h in range(2):
                need("RH", h, p, d)
        for q in range(H // BLK):
            rows = slice(q * BLK, q * BLK + BLK)
            for k in range(16):
                m = rp[k, lax.rem(row, 8) * 16 + yh * 4 + p * (H // BLK) + q].astype(jnp.float32)
                m = jnp.full((BLK, BLK), m).astype(jnp.bfloat16)
                reff[p, rows, k * BLK : k * BLK + BLK] = rbuf[k, p, rows] * m

    def TL1(ph, d):
        rows = pl.ds(d * BLK, BLK)
        send(("TL1", ph, d), t_ref.at[:, pars[ph], xs[2], rows], trel.at[ph, d], x_to[d])

    def TD(ph, d):
        send(("TD", ph, d), t_ref.at[:, pars[ph], xs[(1, 3)[d]]], tbuf.at[ph, x], x_to[d])

    def TL2(ph, d):
        need("TL1", ph, d)
        rows = pl.ds(d * BLK, BLK)
        send(("TL2", ph, d), trel.at[ph, d], tbuf.at[ph, xs[(3, 1)[d]], :, rows], x_to[d])

    def C(p, o, u):
        ph = 1 if o in (0, 3) else 0
        here(("T", ph))
        here(("M", 2))
        for d in range(2):
            need("TD", ph, d)
            need("TL2", ph, d)
        i = lax.div(block[o], 2)
        dst = obuf.at[o, p] if o else out_ref.at[yh, p]
        paths = jnp.dot(reff[p], seff[o, :, cols(u)], preferred_element_type=jnp.float32)
        for h in range(H // BLK):
            q = p * (H // BLK) + h
            for n, c in enumerate(halves(u)):
                m = tp[(block[o] * 4 + x) * 2 + c, lax.rem(row, 8) * 16 + yh * 4 + q]
                t = tbuf[ph, q, i, cols(c)].astype(jnp.float32).T * m.astype(jnp.float32)
                rows = slice(h * BLK, h * BLK + BLK)
                dst[rows, cols(c)] = (paths[rows, cols(n)] * t).astype(jnp.bfloat16)

    def OD(p, o, u):
        send(
            ("OD", p, o, u), obuf.at[o, p, :, cols(u)], out_ref.at[yh, p, :, cols(u)], y_to[o - 1]
        )

    def OL1(p, d, u):
        part = obuf.at[3, p, half[d], cols(u)]
        send(("OL1", p, d, u), part, orel.at[p, d, :, cols(u)], y_to[d])

    def OL2(p, d, u):
        need("OL1", p, d, u)
        dst = out_ref.at[ys[(3, 1)[d]], p, half[d], cols(u)]
        send(("OL2", p, d, u), orel.at[p, d, :, cols(u)], dst, y_to[d])

    barrier = pltpu.get_barrier_semaphore()
    peers = (*x_to, *z_to, *(z_skip if SKIPS else ()), pair, twin, *s_to.values())
    for device in peers:
        pl.semaphore_signal(barrier, inc=1, device_id=device, device_id_type=MESH)
    for c in range(2):
        fetch(("S", c), s_ref.at[:, cols(c)], sbuf.at[yh, c, core, z, yl])
    for p in range(PASSES):
        fetch(("R", p), r_ref.at[yh, p], rbuf.at[col, p])
    for ph in range(2):
        fetch(("T", ph), t_ref.at[:, pars[ph], x], tbuf.at[ph, x])
    lanes = pl.ds(pl.multiple_of(lax.div(row, 8) * BLK, BLK), BLK)
    fetch(("M", 0), rp_ref.at[:, lanes], rp)
    fetch(("M", 1), sp_ref, sp)
    fetch(("M", 2), tp_ref.at[:, lanes], tp)
    pl.semaphore_wait(barrier, len(peers))

    steps = dict(
        SU=SU, Z=Z, SC=SC, SR=SR, RL1=RL1, RY=RY, RL2=RL2, RX=RX, RH=RH, RF=RF, RR=RR,
        TL1=TL1, TD=TD, TL2=TL2, C=C, OD=OD, OL1=OL1, OL2=OL2,
    )
    for step, *where in ORDER:
        steps[step](*where)
    for name in sent:
        if name[0] in ("OD", "OL2"):
            need(*name)
    for copy in sent.values():
        copy.wait_send()


def body(r_vals, s_vals, t_vals, r_pattern, s_pattern, t_pattern):
    hbm = pl.BlockSpec(memory_space=pltpu.HBM)
    bf16 = jnp.bfloat16
    out = pl.pallas_call(
        kernel,
        out_shape=jax.ShapeDtypeStruct((4, PASSES, H, 256), bf16),
        in_specs=[hbm] * 6,
        out_specs=pl.BlockSpec(memory_space=pltpu.VMEM),
        scratch_shapes=[
            pltpu.VMEM((16, PASSES, H, BLK), bf16),
            pltpu.VMEM((PASSES, 2, H // 2, BLK), bf16),
            pltpu.VMEM((4, 2, 2, 8, 2, 64, BLK), bf16),
            pltpu.VMEM((2, 4, 2, 256, BLK), bf16),
            pltpu.VMEM((2, 2, 2, BLK, BLK), bf16),
            pltpu.VMEM((4, PASSES, H, 256), bf16),
            pltpu.VMEM((PASSES, 2, H // 2, 256), bf16),
            pltpu.VMEM((PASSES, H, 2048), bf16),
            pltpu.VMEM((4, 2048, 256), bf16),
            pltpu.SMEM((16, BLK), jnp.int32),
            pltpu.SMEM((16, 32), jnp.int32),
            pltpu.SMEM((32, BLK), jnp.int32),
            pltpu.SemaphoreType.DMA((len(ORDER),)),
            pltpu.SemaphoreType.DMA((len(ORDER),)),
            pltpu.SemaphoreType.DMA((16,)),
            pltpu.SemaphoreType.DMA((9,)),
        ],
        compiler_params=pltpu.CompilerParams(
            collective_id=0, has_side_effects=True, vmem_limit_bytes=48 << 20
        ),
    )(*[pltpu.with_memory_space_constraint(a, pltpu.HBM) for a in (
        r_vals.reshape(4, PASSES, H, BLK),
        s_vals,
        t_vals.reshape(2, 2, 4, 256, BLK),
        r_pattern.T,
        s_pattern,
        t_pattern,
    )])
    return out.reshape(2048, 256)


def solution(mesh):
    placed = (P("row", "col"), P("row", "col"), P(None, ("row", "col")), P(), P(), P())
    return jax.shard_map(
        body, mesh=mesh, in_specs=placed, out_specs=P("row", "col"), check_vma=False
    )
```

```python
import jax
import jax.numpy as jnp
from jax import lax
from jax.experimental import pallas as pl
from jax.experimental.pallas import tpu as pltpu
from jax.sharding import PartitionSpec as P

MESH = pl.DeviceIdType.MESH
BLK = 128
PASSES = 2
H = 512 // PASSES
UNITS = {0: (2,), 1: (0, 1), 2: (0, 1), 3: (0, 1)}
SKIPS = ((1, 0), (1, 1), (2, 0), (2, 1))
ORDER = (
    ("SU", 1, 0, 0), ("TL1", 0, 0), ("SU", 2, 1, 0), ("SU", 2, 0, 0), ("RX", 0, 1, 0),
    ("RL1", 0, 0), ("SU", 1, 1, 0), ("SU", 2, 0, 1), ("TL1", 0, 1), ("RL1", 0, 1), ("SU", 2, 1, 1),
    ("RX", 0, 0, 1), ("RY", 0, 1), ("TD", 0, 0), ("TD", 0, 1), ("TL1", 1, 1), ("RY", 0, 0),
    ("SU", 1, 0, 1), ("Z", 1, 0, 1, 0), ("Z", 1, 0, 1, 1), ("Z", 2, 0, 1, 0), ("TD", 1, 0),
    ("RX", 0, 1, 1), ("RX", 0, 0, 0), ("SU", 3, 0, 0), ("SU", 1, 1, 1), ("Z", 1, 0, 0, 1),
    ("Z", 1, 0, 0, 0), ("RL2", 0, 1), ("SU", 0, 0, 0), ("SU", 3, 1, 0), ("Z", 2, 0, 1, 1),
    ("Z", 2, 0, 0, 0), ("RL2", 0, 0), ("Z", 2, 1, 1, 0), ("RL1", 1, 0), ("Z", 2, 1, 0, 1),
    ("Z", 2, 0, 0, 1), ("RL1", 1, 1), ("RF", 0, 0, 1), ("RX", 2, 0, 1), ("SU", 3, 0, 1),
    ("SU", 3, 1, 1), ("RY", 1, 0), ("RX", 2, 0, 0), ("Z", 1, 0, 3, 1), ("RY", 1, 1),
    ("Z", 1, 0, 3, 0), ("Z", 1, 0, 2, 1), ("RX", 1, 0, 0), ("Z", 1, 0, 2, 0), ("RX", 1, 0, 1),
    ("Z", 1, 1, 1, 1), ("Z", 1, 1, 1, 0), ("RH", 1, 0, 0), ("RF", 0, 0, 0), ("Z", 1, 1, 0, 1),
    ("RH", 1, 0, 1), ("RF", 0, 1, 1), ("Z", 3, 0, 0, 0), ("RH", 0, 0, 1), ("RH", 0, 0, 0),
    ("SU", 0, 0, 1), ("Z", 2, 1, 1, 1), ("TL2", 0, 0), ("RF", 2, 0, 1), ("TL2", 0, 1),
    ("Z", 2, 0, 2, 0), ("Z", 3, 0, 0, 1), ("Z", 2, 0, 3, 1), ("Z", 2, 0, 3, 0), ("Z", 2, 1, 2, 0),
    ("RF", 2, 0, 0), ("RL2", 1, 1), ("Z", 2, 0, 2, 1), ("RL2", 1, 0), ("SC", 1, 0), ("RF", 1, 0, 0),
    ("Z", 3, 1, 0, 0), ("Z", 3, 1, 0, 1), ("RF", 3, 0, 1), ("Z", 1, 1, 3, 1), ("RF", 1, 0, 1),
    ("Z", 1, 1, 0, 0), ("Z", 1, 1, 2, 1), ("Z", 1, 1, 3, 0), ("Z", 1, 1, 2, 0), ("Z", 2, 1, 3, 0),
    ("RF", 3, 0, 0), ("SR", 1, 0), ("Z", 3, 0, 1, 0), ("RX", 2, 1, 1), ("RX", 2, 1, 0),
    ("Z", 3, 0, 1, 1), ("Z", 2, 1, 3, 1), ("RX", 1, 1, 0), ("Z", 2, 1, 0, 0), ("RX", 1, 1, 1),
    ("Z", 2, 1, 2, 1), ("Z", 3, 1, 1, 0), ("SC", 2, 0), ("RH", 0, 1, 0), ("Z", 0, 2, 0, 0),
    ("RH", 1, 1, 0), ("Z", 3, 1, 1, 1), ("Z", 0, 2, 0, 1), ("RH", 1, 1, 1), ("RR", 0),
    ("TL2", 1, 1), ("C", 0, 1, 0), ("SC", 1, 1), ("RH", 0, 1, 1), ("SR", 2, 0), ("Z", 3, 0, 2, 1),
    ("RF", 0, 1, 0), ("Z", 3, 0, 2, 0), ("RF", 2, 1, 1), ("C", 0, 2, 0), ("RF", 2, 1, 0),
    ("SC", 2, 1), ("RF", 1, 1, 0), ("OD", 0, 2, 0), ("RF", 1, 1, 1), ("OD", 0, 1, 0),
    ("Z", 3, 1, 2, 0), ("SR", 1, 1), ("Z", 3, 1, 2, 1), ("RF", 3, 1, 0), ("RF", 3, 1, 1),
    ("TL1", 1, 0), ("TD", 1, 1), ("C", 0, 1, 1), ("Z", 3, 0, 3, 0), ("SR", 2, 1), ("Z", 3, 0, 3, 1),
    ("C", 0, 2, 1), ("OD", 0, 1, 1), ("OD", 0, 2, 1), ("Z", 0, 2, 1, 0), ("Z", 0, 2, 1, 1),
    ("Z", 3, 1, 3, 0), ("Z", 3, 1, 3, 1), ("RR", 1), ("C", 1, 2, 0), ("C", 1, 1, 0),
    ("OD", 1, 2, 0), ("OD", 1, 1, 0), ("TL2", 1, 0), ("SC", 3, 0), ("C", 1, 2, 1),
    ("Z", 0, 2, 2, 0), ("Z", 0, 2, 2, 1), ("OD", 1, 2, 1), ("SC", 3, 1), ("C", 1, 1, 1),
    ("OD", 1, 1, 1), ("SR", 3, 0), ("C", 1, 3, 0), ("SR", 3, 1), ("OL1", 1, 1, 0), ("C", 1, 3, 1),
    ("OL1", 1, 0, 0), ("OL1", 1, 1, 1), ("Z", 0, 2, 3, 1), ("C", 0, 3, 0), ("OL1", 0, 1, 0),
    ("OL1", 0, 0, 0), ("C", 0, 3, 1), ("Z", 0, 2, 3, 0), ("OL1", 1, 0, 1), ("OL1", 0, 1, 1),
    ("OL1", 0, 0, 1), ("SC", 0, 2), ("OL2", 1, 1, 0), ("OL2", 1, 0, 0), ("OL2", 0, 0, 0),
    ("OL2", 1, 1, 1), ("OL2", 0, 1, 0), ("OL2", 1, 0, 1), ("SR", 0, 2), ("OL2", 0, 0, 1),
    ("OL2", 0, 1, 1), ("C", 1, 0, 2), ("C", 0, 0, 2),
)


def kernel(
    r_ref, s_ref, t_ref, rp_ref, sp_ref, tp_ref, out_ref,
    rbuf, rrel, sbuf, tbuf, trel, obuf, orel, reff, seff, rp, sp, tp, ssem, rsem, usem, lsem,
):
    row, col = lax.axis_index("row"), lax.axis_index("col")
    z, yl, core = lax.div(row, 4), lax.rem(lax.div(row, 2), 2), lax.rem(row, 2)
    yh, x = lax.div(col, 4), lax.rem(col, 4)
    xs = [lax.rem(x + d, 4) for d in range(4)]
    ys = [lax.rem(yh + d, 4) for d in range(4)]
    zs = [lax.rem(z + d, 8) for d in range(8)]
    low = yl * 2 + core
    x_to = [(row, yh * 4 + xs[1]), (row, yh * 4 + xs[3])]
    y_to = [(row, ys[1] * 4 + x), (row, ys[3] * 4 + x)]
    z_to = [(zs[1] * 4 + low, col), (zs[7] * 4 + low, col)]
    z_skip = [(zs[2] * 4 + low, col), (zs[6] * 4 + low, col)]
    pair = (z * 4 + (1 - yl) * 2 + core, col)
    twin = (row + 1 - 2 * core, col)
    s_to = {
        (o, q): (z * 4 + q * 2 + core, ys[d] * 4 + x) for o, d in ((1, 3), (2, 1), (3, 2)) for q in range(2)
    }
    par = lax.rem(yh, 2)
    pars = [1 - par, par]
    block = [yh, ys[1], ys[3], ys[2]]
    half = [pl.ds(0, H // 2), pl.ds(H // 2, H // 2)]

    sent, seen, local = {}, set(), {}

    def send(name, src, dst, device, arrival=None):
        n = len(sent)
        sent[name] = pltpu.make_async_remote_copy(
            src_ref=src, dst_ref=dst, send_sem=ssem.at[n],
            recv_sem=rsem.at[n] if arrival is None else usem.at[arrival],
            device_id=device, device_id_type=MESH,
        )
        sent[name].start()

    def need(*name):
        if name not in seen:
            seen.add(name)
            sent[name].wait_recv()

    def here(name):
        if name not in seen:
            seen.add(name)
            local[name].wait()

    def fetch(name, src, dst):
        local[name] = pltpu.make_async_copy(src, dst, lsem.at[len(local)])
        local[name].start()

    def cols(u):
        return slice(0, 256) if u == 2 else slice(u * BLK, u * BLK + BLK)

    def halves(u):
        return (0, 1) if u == 2 else (u,)

    def SU(o, q, c):
        src, dst = s_ref.at[:, cols(c)], sbuf.at[yh, c, core, z, yl]
        if o:
            send(("SU", o, q, c), src, dst, s_to[o, q], (o * 2 + yl) * 2 + c)
        else:
            send(("SU", o, q, c), src, dst, pair, c)

    def s_came(o, c):
        for q in range(2 if o else 1):
            if ("SU", o, q, c) in seen:
                continue
            seen.add(("SU", o, q, c))
            part = sbuf.at[block[o], c, core, z, q]
            pltpu.make_async_remote_copy(
                src_ref=part, dst_ref=part, send_sem=ssem.at[0], recv_sem=usem.at[(o * 2 + q) * 2 + c],
                device_id=pair, device_id_type=MESH,
            ).wait_recv()

    def Z(o, u, s, d):
        skip = (o, u) in SKIPS
        back = (0, 0, 2, 2)[s] if skip else s
        if back:
            need("Z", o, u, back - 1, d)
        else:
            for c in halves(u):
                s_came(o, c)
                if o == 0:
                    here(("S", c))
        part = sbuf.at[block[o], slice(0, 2) if u == 2 else u, core, zs[(-back, back)[d]]]
        if s == 3:
            part = part.at[:, d] if u == 2 else part.at[d]
        send(("Z", o, u, s, d), part, part, (z_skip if skip and s in (1, 3) else z_to)[d])

    def SC(o, u):
        for d in range(2):
            for s in range(4):
                need("Z", o, u, s, d)
        part = sbuf.at[block[o], slice(0, 2) if u == 2 else u, core]
        send(("SC", o, u), part, part, twin)

    def SR(o, u):
        need("SC", o, u)
        here(("M", 1))
        j = (block[o] * 4 + x) * 2
        for k in range(16):
            for c in halves(u):
                m = jnp.full((64, BLK), sp[k, j + c].astype(jnp.float32)).astype(jnp.bfloat16)
                for b in range(2):
                    rows = slice(k * 128 + b * 64, k * 128 + b * 64 + 64)
                    seff[o, rows, cols(c)] = sbuf[block[o], c, b, k // 2, k % 2] * m

    def RL1(p, d):
        send(("RL1", p, d), r_ref.at[ys[2], p, half[d]], rrel.at[p, d], y_to[d])

    def RY(p, d):
        send(("RY", p, d), r_ref.at[ys[(1, 3)[d]], p], rbuf.at[col, p], y_to[d])

    def RL2(p, d):
        need("RL1", p, d)
        send(("RL2", p, d), rrel.at[p, d], rbuf.at[ys[(3, 1)[d]] * 4 + x, p, half[d]], y_to[d])

    def RX(j, p, d):
        part = rbuf.at[ys[(0, 3, 1, 2)[j]] * 4 + x, p]
        if j == 0:
            send(("RX", j, p, d), r_ref.at[yh, p], part, x_to[d])
            return
        need("RY", p, j - 1)
        send(("RX", j, p, d), part, part, x_to[d])

    def RH(h, p, d):
        need("RL2", p, h)
        part = rbuf.at[ys[2] * 4 + x, p, half[h]]
        send(("RH", h, p, d), part, part, x_to[d])

    def RF(j, p, d):
        if j == 3:
            need("RH", d, p, d)
        else:
            need("RX", j, p, d)
        part = rbuf.at[ys[(0, 3, 1, 2)[j]] * 4 + xs[(3, 1)[d]], p, half[d]]
        send(("RF", j, p, d), part, part, x_to[d])

    def RR(p):
        here(("R", p))
        here(("M", 0))
        for d in range(2):
            need("RY", p, d)
            need("RL2", p, d)
            for j in range(4):
                if j < 3:
                    need("RX", j, p, d)
                need("RF", j, p, d)
            for h in range(2):
                need("RH", h, p, d)
        for q in range(H // BLK):
            rows = slice(q * BLK, q * BLK + BLK)
            for k in range(16):
                m = rp[k, lax.rem(row, 8) * 16 + yh * 4 + p * (H // BLK) + q].astype(jnp.float32)
                m = jnp.full((BLK, BLK), m).astype(jnp.bfloat16)
                reff[p, rows, k * BLK : k * BLK + BLK] = rbuf[k, p, rows] * m

    def TL1(ph, d):
        rows = pl.ds(d * BLK, BLK)
        send(("TL1", ph, d), t_ref.at[:, pars[ph], xs[2], rows], trel.at[ph, d], x_to[d])

    def TD(ph, d):
        send(("TD", ph, d), t_ref.at[:, pars[ph], xs[(1, 3)[d]]], tbuf.at[ph, x], x_to[d])

    def TL2(ph, d):
        need("TL1", ph, d)
        rows = pl.ds(d * BLK, BLK)
        send(("TL2", ph, d), trel.at[ph, d], tbuf.at[ph, xs[(3, 1)[d]], :, rows], x_to[d])

    def C(p, o, u):
        ph = 1 if o in (0, 3) else 0
        here(("T", ph))
        here(("M", 2))
        for d in range(2):
            need("TD", ph, d)
            need("TL2", ph, d)
        i = lax.div(block[o], 2)
        dst = obuf.at[o, p] if o else out_ref.at[yh, p]
        paths = jnp.dot(reff[p], seff[o, :, cols(u)], preferred_element_type=jnp.float32)
        for h in range(H // BLK):
            q = p * (H // BLK) + h
            for n, c in enumerate(halves(u)):
                m = tp[(block[o] * 4 + x) * 2 + c, lax.rem(row, 8) * 16 + yh * 4 + q]
                t = tbuf[ph, q, i, cols(c)].astype(jnp.float32).T * m.astype(jnp.float32)
                rows = slice(h * BLK, h * BLK + BLK)
                dst[rows, cols(c)] = (paths[rows, cols(n)] * t).astype(jnp.bfloat16)

    def OD(p, o, u):
        send(
            ("OD", p, o, u), obuf.at[o, p, :, cols(u)], out_ref.at[yh, p, :, cols(u)], y_to[o - 1]
        )

    def OL1(p, d, u):
        part = obuf.at[3, p, half[d], cols(u)]
        send(("OL1", p, d, u), part, orel.at[p, d, :, cols(u)], y_to[d])

    def OL2(p, d, u):
        need("OL1", p, d, u)
        dst = out_ref.at[ys[(3, 1)[d]], p, half[d], cols(u)]
        send(("OL2", p, d, u), orel.at[p, d, :, cols(u)], dst, y_to[d])

    barrier = pltpu.get_barrier_semaphore()
    peers = (*x_to, *z_to, *(z_skip if SKIPS else ()), pair, twin, *s_to.values())
    for device in peers:
        pl.semaphore_signal(barrier, inc=1, device_id=device, device_id_type=MESH)
    for c in range(2):
        fetch(("S", c), s_ref.at[:, cols(c)], sbuf.at[yh, c, core, z, yl])
    for p in range(PASSES):
        fetch(("R", p), r_ref.at[yh, p], rbuf.at[col, p])
    for ph in range(2):
        fetch(("T", ph), t_ref.at[:, pars[ph], x], tbuf.at[ph, x])
    lanes = pl.ds(pl.multiple_of(lax.div(row, 8) * BLK, BLK), BLK)
    fetch(("M", 0), rp_ref.at[:, lanes], rp)
    fetch(("M", 1), sp_ref, sp)
    fetch(("M", 2), tp_ref.at[:, lanes], tp)
    pl.semaphore_wait(barrier, len(peers))

    steps = dict(
        SU=SU, Z=Z, SC=SC, SR=SR, RL1=RL1, RY=RY, RL2=RL2, RX=RX, RH=RH, RF=RF, RR=RR,
        TL1=TL1, TD=TD, TL2=TL2, C=C, OD=OD, OL1=OL1, OL2=OL2,
    )
    for step, *where in ORDER:
        steps[step](*where)
    for name in sent:
        if name[0] in ("OD", "OL2"):
            need(*name)
    for copy in sent.values():
        copy.wait_send()


def body(r_vals, s_vals, t_vals, r_pattern, s_pattern, t_pattern):
    hbm = pl.BlockSpec(memory_space=pltpu.HBM)
    bf16 = jnp.bfloat16
    out = pl.pallas_call(
        kernel,
        out_shape=jax.ShapeDtypeStruct((4, PASSES, H, 256), bf16),
        in_specs=[hbm] * 6,
        out_specs=pl.BlockSpec(memory_space=pltpu.VMEM),
        scratch_shapes=[
            pltpu.VMEM((16, PASSES, H, BLK), bf16),
            pltpu.VMEM((PASSES, 2, H // 2, BLK), bf16),
            pltpu.VMEM((4, 2, 2, 8, 2, 64, BLK), bf16),
            pltpu.VMEM((2, 4, 2, 256, BLK), bf16),
            pltpu.VMEM((2, 2, 2, BLK, BLK), bf16),
            pltpu.VMEM((4, PASSES, H, 256), bf16),
            pltpu.VMEM((PASSES, 2, H // 2, 256), bf16),
            pltpu.VMEM((PASSES, H, 2048), bf16),
            pltpu.VMEM((4, 2048, 256), bf16),
            pltpu.SMEM((16, BLK), jnp.int32),
            pltpu.SMEM((16, 32), jnp.int32),
            pltpu.SMEM((32, BLK), jnp.int32),
            pltpu.SemaphoreType.DMA((len(ORDER),)),
            pltpu.SemaphoreType.DMA((len(ORDER),)),
            pltpu.SemaphoreType.DMA((16,)),
            pltpu.SemaphoreType.DMA((9,)),
        ],
        compiler_params=pltpu.CompilerParams(
            collective_id=0, has_side_effects=True, vmem_limit_bytes=48 << 20
        ),
    )(*[pltpu.with_memory_space_constraint(a, pltpu.HBM) for a in (
        r_vals.reshape(4, PASSES, H, BLK),
        s_vals,
        t_vals.reshape(2, 2, 4, 256, BLK),
        r_pattern.T,
        s_pattern,
        t_pattern,
    )])
    return out.reshape(2048, 256)


def solution(mesh):
    placed = (P("row", "col"), P("row", "col"), P(None, ("row", "col")), P(), P(), P())
    return jax.shard_map(
        body, mesh=mesh, in_specs=placed, out_specs=P("row", "col"), check_vma=False
    )
```
